32 devices in a mesh: groups: 2 (over x), dp: 16 (over z, y, core).
Axes of the slice: x: 2, y: 2, z: 4, core: 2. Of those that a mesh axis runs over, the one named last changes fastest.
Arguments:
- states: bfloat16 [16384, 1024], P(('groups', 'dp')), parts along dimension 0, may hold values from -6 to 6
- lengths: int32 [64], P(('groups', 'dp')), parts along dimension 0, may hold values from 1 to 256, as said below
- norm_gain: bfloat16 [1024], replicated, may hold values from 0.5 to 2
- w_gate: bfloat16 [1024, 1536], replicated, may hold values from -0.1875 to 0.1875
- w_up: bfloat16 [1024, 1536], replicated, may hold values from -0.1875 to 0.1875
- w_down: bfloat16 [1536, 1024], replicated, may hold values from -0.15625 to 0.15625
- context: bfloat16 [64, 4096], P('groups', 'dp'), parts along dimension 0, may hold values from -6 to 6
- w_out: bfloat16 [4096, 4096], P('dp'), may hold values from -0.09375 to 0.09375
- resid_stream: bfloat16 [64, 4096], P('groups'), parts along dimension 0, may hold values from -6 to 6
- teacher_gain: bfloat16 [4096], replicated, may hold values from 0.5 to 2
Outputs:
- gram_loss: float32 [2], P('groups'), parts along dimension 0
- grad_gate: float32 [2048, 1536], P(('groups', 'dp')), parts along dimension 0
- grad_up: float32 [2048, 1536], P(('groups', 'dp')), parts along dimension 0
- grad_down: float32 [3072, 1024], P(('groups', 'dp')), parts along dimension 0
The draws below stay inside these ranges and needn't reach their ends.
There are 2 independent parts, one for each index of `groups`. The reference program is written for one: setup_inputs(seed, part) draws one part's arguments, and reference() takes and returns one part's arrays. A program takes and returns all parts, laid end to end along the dimension named above; an argument that names none is the same for every part. Nothing has to cross between parts.
Inputs may be any that keep to these rules, and one draw needn't show every extreme that they name: `lengths`: some document of every group fills all 256 slots and some has a single valid token.
All inputs are finite; a program needn't handle non-finite values.
Results may differ from the reference program's by a relative error of at most 0.004.
Values may be sent and summed in bfloat16 or wider, within the bound.
A program may use at most 128 MiB of HBM per device.

```python
import math
import jax
import jax.numpy as jnp
from jax import lax

SD = 1024
FF = 1536
TD = 4096
SEQ = 256
DOCS = 32
TOKENS = 8192


def draw_lengths(key, part):
    drawn_lengths = jax.random.randint(key, (DOCS,), 1, SEQ + 1)
    full_index = jax.random.randint(jax.random.fold_in(key, 7), (), 0, DOCS)
    positions = jnp.arange(DOCS, dtype=jnp.int32)
    drawn_lengths = jnp.where(positions == full_index, SEQ, drawn_lengths)
    drawn_lengths = jnp.where(positions == (full_index + 1) % DOCS, 1, drawn_lengths)
    return drawn_lengths.astype(jnp.int32)


def steps_of(key, extent, shards, low, largest):
    def one(axis_at, shards_of):
        steps = jax.random.uniform(jax.random.fold_in(jax.random.fold_in(key, 6), axis_at), (shards_of,), jnp.float32, low / len(shards), largest / len(shards))
        return jnp.repeat(jnp.exp(steps), extent[axis_at] // shards_of).reshape((-1,) + (1,) * (len(extent) - axis_at - 1))

    factor_of = one(*shards[0])
    for cut in shards[1:]:
        factor_of = factor_of * one(*cut)
    return factor_of


def scatter_about(rng, extent, deviation, limit, cuts=(), held_as=jnp.bfloat16):
    entries = jax.random.normal(rng, extent, jnp.float32) * deviation
    if len(cuts) > 0:
        entries = steps_of(rng, extent, cuts, -0.22, 0.18) * entries
    return jnp.clip(entries, min=-limit, max=limit).astype(held_as)


def setup_inputs(seed: int = 0, part: int = 0) -> dict:
    splits = jax.random.split(jax.random.key(seed), 11)
    own_keys = jax.random.split(jax.random.fold_in(splits[10], part), 11)
    states = scatter_about(own_keys[0], (TOKENS, SD), 1.0, 6.0, ((0, 16),))
    lengths = draw_lengths(jax.random.fold_in(jax.random.fold_in(splits[10], part), 71), part)
    norm_gain = jnp.clip(jnp.exp(jax.random.uniform(splits[2], (SD,), jnp.float32, math.log(0.5), math.log(2.0))), 0.5, 2.0).astype(jnp.bfloat16)
    w_gate = scatter_about(splits[3], (SD, FF), SD ** -0.5, 0.1875)
    w_up = scatter_about(splits[4], (SD, FF), SD ** -0.5, 0.1875)
    w_down = scatter_about(splits[5], (FF, SD), FF ** -0.5, 0.15625)
    context = scatter_about(own_keys[6], (DOCS, TD), 1.0, 6.0, ((1, 16),))
    w_out = scatter_about(splits[7], (TD, TD), TD ** -0.5, 0.09375, ((0, 16),))
    resid_stream = scatter_about(own_keys[8], (DOCS, TD), 1.0, 6.0)
    teacher_gain = jnp.clip(jnp.exp(jax.random.uniform(splits[9], (TD,), jnp.float32, math.log(0.5), math.log(2.0))), 0.5, 2.0).astype(jnp.bfloat16)
    return dict(states=states, lengths=lengths, norm_gain=norm_gain, w_gate=w_gate, w_up=w_up, w_down=w_down, context=context, w_out=w_out, resid_stream=resid_stream, teacher_gain=teacher_gain)


EPS = 1e-06
LOSS_SCALE = 4096.0

def teacher_embed(attn_rows, resid_rows, teacher_gain):
    scaled_rows = teacher_gain.astype(jnp.float32) * (resid_rows.astype(jnp.float32) + attn_rows)
    inv_teacher = lax.rsqrt(lax.optimization_barrier(jnp.sum(scaled_rows * scaled_rows, axis=1, keepdims=True)) + EPS)
    return (scaled_rows * inv_teacher).astype(jnp.bfloat16)

def reference(states, lengths, norm_gain, w_gate, w_up, w_down, context, w_out, resid_stream, teacher_gain):
    attn_rows = jnp.dot(context, w_out, preferred_element_type=jnp.float32)
    teacher_rows = teacher_embed(attn_rows, resid_stream, teacher_gain)
    gram_teacher = jnp.dot(teacher_rows, teacher_rows.T, preferred_element_type=jnp.float32)
    states_wide = states.astype(jnp.float32)
    inv_rms = lax.rsqrt(lax.optimization_barrier(jnp.mean(states_wide * states_wide, axis=1, keepdims=True)) + EPS)
    normed = (states_wide * inv_rms * norm_gain.astype(jnp.float32)).astype(jnp.bfloat16)
    gate_pre = jnp.dot(normed, w_gate, preferred_element_type=jnp.float32)
    up_pre = jnp.dot(normed, w_up, preferred_element_type=jnp.float32)
    hidden = (jax.nn.silu(gate_pre) * up_pre).astype(jnp.bfloat16)
    layer_out = states_wide + jnp.dot(hidden, w_down, preferred_element_type=jnp.float32)
    positions = jnp.arange(SEQ, dtype=jnp.int32)
    valid_mask = (positions[None, :] < lengths[:, None]).astype(jnp.float32)
    counts = lengths.astype(jnp.float32)
    pooled = lax.optimization_barrier(jnp.sum(layer_out.reshape(DOCS, SEQ, SD) * valid_mask[:, :, None], axis=1)) / counts[:, None]
    inv_norm = lax.rsqrt(lax.optimization_barrier(jnp.sum(pooled * pooled, axis=1, keepdims=True)) + EPS)
    unit_rows = pooled * inv_norm
    embed_rows = unit_rows.astype(jnp.bfloat16)
    gram_student = jnp.dot(embed_rows, embed_rows.T, preferred_element_type=jnp.float32)
    gram_diff = gram_student - gram_teacher
    diff_norm = jnp.sqrt(jnp.sum(gram_diff * gram_diff) + EPS)
    teacher_norm = jnp.sqrt(jnp.sum(gram_teacher * gram_teacher))
    gram_loss = diff_norm / teacher_norm
    d_gram = LOSS_SCALE * gram_diff / (diff_norm * teacher_norm)
    d_embed = 2.0 * jnp.dot(d_gram, embed_rows.astype(jnp.float32), precision=lax.Precision.HIGHEST)
    along = lax.optimization_barrier(jnp.sum(unit_rows * d_embed, axis=1, keepdims=True))
    d_pooled = (d_embed - unit_rows * along) * inv_norm
    d_doc = (d_pooled / counts[:, None]).astype(jnp.bfloat16)
    d_token = (d_doc.astype(jnp.float32)[:, None, :] * valid_mask[:, :, None]).astype(jnp.bfloat16).reshape(TOKENS, SD)
    grad_down = jnp.dot(hidden.T, d_token, preferred_element_type=jnp.float32)
    d_hidden = jnp.dot(d_doc, w_down.T, preferred_element_type=jnp.float32)
    d_hidden_tok = (d_hidden[:, None, :] * valid_mask[:, :, None]).reshape(TOKENS, FF)
    sigmoid_gate = jax.nn.sigmoid(gate_pre)
    d_gate = (d_hidden_tok * up_pre * sigmoid_gate * (1.0 + gate_pre * (1.0 - sigmoid_gate))).astype(jnp.bfloat16)
    d_up = (d_hidden_tok * jax.nn.silu(gate_pre)).astype(jnp.bfloat16)
    grad_gate = jnp.dot(normed.T, d_gate, preferred_element_type=jnp.float32)
    grad_up = jnp.dot(normed.T, d_up, preferred_element_type=jnp.float32)
    return (gram_loss.reshape(1), grad_gate, grad_up, grad_down)
```

```python
import jax
import jax.numpy as jnp
from jax import lax
from jax.sharding import PartitionSpec as P

EPS = 1e-06
LOSS_SCALE = 4096.0


def teacher_embed(attn_rows, resid_rows, teacher_gain):
    scaled_rows = teacher_gain.astype(jnp.float32) * (resid_rows.astype(jnp.float32) + attn_rows)
    inv_teacher = lax.rsqrt(jnp.sum(scaled_rows * scaled_rows, axis=1, keepdims=True) + EPS)
    return (scaled_rows * inv_teacher).astype(jnp.bfloat16)


def rows_product(left_rows, right_rows):
    return lax.dot_general(
        left_rows, right_rows, (((1,), (1,)), ((), ())), preferred_element_type=jnp.float32
    )


def cols_product(left_cols, right_cols):
    return lax.dot_general(
        left_cols, right_cols, (((0,), (0,)), ((), ())), preferred_element_type=jnp.float32
    )


def per_device(
    states, lengths, norm_gain, w_gate, w_up, w_down, context, w_out, resid_stream, teacher_gain
):
    dp = lax.axis_size("dp")
    my_index = lax.axis_index("dp")
    doc_dev = lengths.shape[0]
    seq_len = states.shape[0] // doc_dev
    model_width = states.shape[1]
    hidden_width = w_gate.shape[1]
    feat = w_out.shape[1] // dp
    high = lax.Precision.HIGHEST
    partial_attn = jnp.dot(context, w_out, preferred_element_type=jnp.float32)
    attn_cols = lax.psum_scatter(partial_attn, "dp", scatter_dimension=1, tiled=True)
    resid_cols = lax.dynamic_slice_in_dim(resid_stream, my_index * feat, feat, 1)
    gain_cols = lax.dynamic_slice_in_dim(teacher_gain, my_index * feat, feat, 0)
    scaled = gain_cols.astype(jnp.float32) * (resid_cols.astype(jnp.float32) + attn_cols)
    gram_part = lax.dot_general(scaled, scaled, (((1,), (1,)), ((), ())), precision=high)
    states_wide = states.astype(jnp.float32)
    inv_rms = lax.rsqrt(jnp.mean(states_wide * states_wide, axis=1, keepdims=True) + EPS)
    normed = (states_wide * inv_rms * norm_gain.astype(jnp.float32)).astype(jnp.bfloat16)
    gate_pre = jnp.dot(normed, w_gate, preferred_element_type=jnp.float32)
    up_pre = jnp.dot(normed, w_up, preferred_element_type=jnp.float32)
    hidden = (jax.nn.silu(gate_pre) * up_pre).astype(jnp.bfloat16)
    positions = lax.broadcasted_iota(jnp.int32, (doc_dev, seq_len), 1)
    valid_mask = (positions < lengths[:, None]).astype(jnp.float32)
    counts = lengths.astype(jnp.float32)
    hidden_sum = jnp.sum(
        hidden.astype(jnp.float32).reshape(doc_dev, seq_len, hidden_width) * valid_mask[:, :, None], axis=1
    )
    state_sum = jnp.sum(states_wide.reshape(doc_dev, seq_len, model_width) * valid_mask[:, :, None], axis=1)
    packed = jnp.concatenate([hidden_sum, state_sum, jnp.broadcast_to(counts[:, None], (doc_dev, 128))], axis=1)
    packed_all = lax.all_gather(packed, "dp", axis=0, tiled=True)
    hidden_all = packed_all[:, :hidden_width]
    state_all = packed_all[:, hidden_width : hidden_width + model_width]
    count_all = packed_all[:, hidden_width + model_width :][:, :1]
    gram_raw = lax.psum(gram_part, "dp")
    docs = gram_raw.shape[0]
    eye = jnp.eye(docs, dtype=jnp.float32)
    inv_col = lax.rsqrt(jnp.sum(gram_raw * eye, axis=1, keepdims=True) + EPS)
    inv_row = lax.rsqrt(jnp.sum(gram_raw * eye, axis=0, keepdims=True) + EPS)
    gram_teacher = gram_raw * inv_col * inv_row
    pooled = (state_all + jnp.dot(hidden_all, w_down.astype(jnp.float32), precision=high)) / count_all
    inv_norm = lax.rsqrt(jnp.sum(pooled * pooled, axis=1, keepdims=True) + EPS)
    unit_rows = pooled * inv_norm
    embed = unit_rows.astype(jnp.bfloat16)
    gram_diff = rows_product(embed, embed) - gram_teacher
    diff_norm = jnp.sqrt(jnp.sum(gram_diff * gram_diff) + EPS)
    teacher_norm = jnp.sqrt(jnp.sum(gram_teacher * gram_teacher))
    gram_loss = (diff_norm / teacher_norm).reshape(1)
    d_gram = LOSS_SCALE * gram_diff / (diff_norm * teacher_norm)
    d_embed = 2.0 * jnp.dot(d_gram, embed.astype(jnp.float32), precision=high)
    along = jnp.sum(unit_rows * d_embed, axis=1, keepdims=True)
    d_pooled = (d_embed - unit_rows * along) * inv_norm
    d_all = (d_pooled / count_all).astype(jnp.bfloat16)
    down_rows = hidden_width // dp
    own_hidden = lax.dynamic_slice_in_dim(hidden_all, my_index * down_rows, down_rows, 1)
    grad_down = lax.dot_general(
        own_hidden, d_all.astype(jnp.float32), (((0,), (0,)), ((), ())), precision=high
    )
    d_doc = lax.dynamic_slice_in_dim(d_all, my_index * doc_dev, doc_dev, 0)
    d_hidden = rows_product(d_doc, w_down)
    d_hidden_tok = (d_hidden[:, None, :] * valid_mask[:, :, None]).reshape(
        doc_dev * seq_len, hidden_width
    )
    sigmoid_gate = jax.nn.sigmoid(gate_pre)
    d_gate = (
        d_hidden_tok * up_pre * sigmoid_gate * (1.0 + gate_pre * (1.0 - sigmoid_gate))
    ).astype(jnp.bfloat16)
    d_up = (d_hidden_tok * jax.nn.silu(gate_pre)).astype(jnp.bfloat16)
    rows = model_width // dp
    terms = jnp.concatenate([cols_product(normed, d_gate), cols_product(normed, d_up)], axis=1)
    terms = terms.astype(jnp.bfloat16)
    swapped = lax.all_to_all(terms.reshape(dp, rows, 2 * hidden_width), "dp", 0, 0)
    total = jnp.sum(swapped.astype(jnp.float32), axis=0)
    return (gram_loss, total[:, :hidden_width], total[:, hidden_width:], grad_down)


def solution(mesh):
    in_specs = (
        P(("groups", "dp"), None),
        P(("groups", "dp")),
        P(),
        P(),
        P(),
        P(),
        P("groups", "dp"),
        P("dp", None),
        P("groups", None),
        P(),
    )
    out_specs = (
        P("groups"),
        P(("groups", "dp"), None),
        P(("groups", "dp"), None),
        P(("groups", "dp"), None),
    )
    return jax.shard_map(
        per_device, mesh=mesh, in_specs=in_specs, out_specs=out_specs, check_vma=False
    )
```

```python
import functools

import jax
import jax.numpy as jnp
from jax import lax
from jax.experimental import pallas as pl
from jax.experimental.pallas import tpu as pltpu
from jax.sharding import PartitionSpec as P

EPS = 1e-06
LOSS_SCALE = 4096.0
MESH = pl.DeviceIdType.MESH
F32 = jnp.float32
BF16 = jnp.bfloat16


def rows_product(left_rows, right_rows):
    return lax.dot_general(
        left_rows, right_rows, (((1,), (1,)), ((), ())), preferred_element_type=F32
    )


def split3(wide):
    high = wide.astype(BF16)
    rest = wide - high.astype(F32)
    middle = rest.astype(BF16)
    low = (rest - middle.astype(F32)).astype(BF16)
    return high, middle, low


def step_kernel(
    n, width,
    states, lengths, norm_gain, w_gate, w_up, w_down, context, w_out, resid, gain,
    loss_out, gate_out, up_out, down_out,
    t_send, t_recv, g_all, p_all, big, feats, feats_in, acts, d_hid,
    y_send, y_part, y_recv, z_send, z_recv, z_part,
    t_ssem, t_rsem, g_ssem, g_rsem, p_ssem, p_rsem, s_ssem, s_rsem,
    y_ssem, y_rsem, z_ssem, z_rsem,
):
    me = lax.axis_index("dp")
    core = lax.rem(me, 2)
    row = lax.rem(lax.div(me, 2), 2)
    col = lax.div(me, 4)
    cols = n // 4
    sibling = me + 1 - 2 * core
    across = me + 2 - 4 * row
    docs_dev = lengths.shape[0]
    tokens, model = states.shape
    seq = tokens // docs_dev
    hidden_width = w_gate.shape[1]
    docs = context.shape[0]
    feat = w_out.shape[1] // n
    rows = model // n
    down_rows = hidden_width // n
    pieces = hidden_width // width
    chunks = 2 * pieces

    def peer(d):
        return lax.rem(me + d, n)

    barrier = pltpu.get_barrier_semaphore()

    @pl.loop(1, n)
    def _(d):
        pl.semaphore_signal(barrier, inc=1, device_id={"dp": peer(d)}, device_id_type=MESH)

    partial = jnp.dot(context[...], w_out[...], preferred_element_type=F32)
    first = (me == 0).astype(F32)
    partial = gain[...].astype(F32) * (partial + first * resid[...].astype(F32))
    for j in range(n):
        t_send[j] = partial[:, j * feat : (j + 1) * feat].astype(BF16)
    t_recv[me] = t_send[me]
    pl.semaphore_wait(barrier, n - 1)

    def t_copy(dst, src):
        return pltpu.make_async_remote_copy(
            src_ref=t_send.at[dst], dst_ref=t_recv.at[src], send_sem=t_ssem.at[dst],
            recv_sem=t_rsem.at[src], device_id={"dp": dst}, device_id_type=MESH,
        )

    @pl.loop(1, n)
    def _(d):
        t_copy(peer(d), me).start()

    normed_parts = []
    masks = []
    for d in range(docs_dev):
        x = states[d * seq : (d + 1) * seq].astype(F32)
        inv_rms = lax.rsqrt(jnp.mean(x * x, axis=1, keepdims=True) + EPS)
        normed_wide = x * inv_rms * norm_gain[...].astype(F32)
        normed = normed_wide.astype(BF16)
        normed_parts.append(normed)
        turned = normed.astype(F32).T.astype(BF16)
        feats[:, :, :, :, d * seq : (d + 1) * seq] = turned.reshape(cols, 2, 2, rows, seq)
        length = lengths[d]
        mask = (lax.broadcasted_iota(jnp.int32, (seq, 1), 0) < length).astype(F32)
        masks.append(mask)
        p_all[me, d : d + 1, hidden_width : hidden_width + model] = jnp.sum(
            x * mask, axis=0, keepdims=True
        )
        p_all[me, d : d + 1, hidden_width + model :] = jnp.zeros((1, 128), F32) + length.astype(F32)
    normed = jnp.concatenate(normed_parts, axis=0)
    mask = jnp.concatenate(masks, axis=0)

    feats_copy = pltpu.make_async_remote_copy(
        src_ref=feats.at[:, :, 1 - core], dst_ref=feats_in, send_sem=s_ssem.at[chunks],
        recv_sem=s_rsem.at[chunks], device_id={"dp": sibling}, device_id_type=MESH,
    )
    feats_copy.start()

    def acts_copy(c):
        return pltpu.make_async_remote_copy(
            src_ref=acts.at[0, c], dst_ref=acts.at[1, c], send_sem=s_ssem.at[c],
            recv_sem=s_rsem.at[c], device_id={"dp": sibling}, device_id_type=MESH,
        )

    @pl.loop(0, pieces)
    def _(c):
        at = pl.ds(pl.multiple_of(c * width, width), width)
        gate_pre = jnp.dot(normed, w_gate[:, at], preferred_element_type=F32)
        up_pre = jnp.dot(normed, w_up[:, at], preferred_element_type=F32)
        sig = jax.nn.sigmoid(gate_pre)
        silu = gate_pre * sig
        hidden = (silu * up_pre).astype(BF16).astype(F32) * mask
        for d in range(docs_dev):
            p_all[me, d : d + 1, at] = jnp.sum(
                hidden[d * seq : (d + 1) * seq], axis=0, keepdims=True
            )
        acts[0, c] = (mask * up_pre * sig * (1.0 + gate_pre * (1.0 - sig))).astype(BF16)
        acts[0, c + pieces] = (mask * silu).astype(BF16)

    def p_copy(dst, src):
        return pltpu.make_async_remote_copy(
            src_ref=p_all.at[src], dst_ref=p_all.at[src], send_sem=p_ssem.at[dst],
            recv_sem=p_rsem.at[src], device_id={"dp": dst}, device_id_type=MESH,
        )

    def g_copy(dst, src):
        return pltpu.make_async_remote_copy(
            src_ref=g_all.at[src], dst_ref=g_all.at[src], send_sem=g_ssem.at[dst],
            recv_sem=g_rsem.at[src], device_id={"dp": dst}, device_id_type=MESH,
        )

    @pl.loop(1, n)
    def _(d):
        p_copy(peer(d), me).start()

    @pl.loop(1, n)
    def _(d):
        t_copy(me, peer(d)).wait_recv()

    scaled = jnp.sum(t_recv[...].astype(F32), axis=0)
    gram_part = lax.dot_general(
        scaled, scaled, (((1,), (1,)), ((), ())), precision=lax.Precision.HIGHEST,
        preferred_element_type=F32,
    )
    fold = max(1, 128 // docs)
    fold_rows = docs // fold
    g_all[me] = jnp.concatenate(
        [gram_part[i * fold_rows : (i + 1) * fold_rows] for i in range(fold)], axis=1
    )

    @pl.loop(1, n)
    def _(d):
        g_copy(peer(d), me).start()

    @pl.loop(0, chunks)
    def _(c):
        acts_copy(c).start()

    @pl.loop(1, n)
    def _(d):
        p_copy(me, peer(d)).wait_recv()

    for j in range(n):
        big[j * docs_dev : (j + 1) * docs_dev, :] = p_all[j]
    sums = jnp.concatenate(split3(big[:, :hidden_width]), axis=0)
    count_all = big[:, hidden_width + model : hidden_width + model + 1]
    lifted = jnp.dot(sums, w_down[...], preferred_element_type=F32)
    lifted = lifted[:docs] + (lifted[docs : 2 * docs] + lifted[2 * docs :])
    pooled = (big[:, hidden_width : hidden_width + model] + lifted) / count_all
    inv_norm = lax.rsqrt(jnp.sum(pooled * pooled, axis=1, keepdims=True) + EPS)
    unit_rows = pooled * inv_norm
    embed = unit_rows.astype(BF16)
    gram_student = rows_product(embed, embed)

    @pl.loop(1, n)
    def _(d):
        g_copy(me, peer(d)).wait_recv()

    folded = jnp.sum(g_all[...], axis=0)
    gram_raw = jnp.concatenate(
        [folded[:, i * docs : (i + 1) * docs] for i in range(fold)], axis=0
    )
    diagonal = lax.broadcasted_iota(jnp.int32, (docs, docs), 0) == lax.broadcasted_iota(
        jnp.int32, (docs, docs), 1
    )
    squares = jnp.where(diagonal, gram_raw, 0.0)
    inv_col = lax.rsqrt(jnp.sum(squares, axis=1, keepdims=True) + EPS)
    inv_row = lax.rsqrt(jnp.sum(squares, axis=0, keepdims=True) + EPS)
    gram_teacher = gram_raw * inv_col * inv_row
    gram_diff = gram_student - gram_teacher

    def total(square):
        return jnp.sum(jnp.sum(square, axis=1, keepdims=True), axis=0, keepdims=True)

    diff_norm = jnp.sqrt(total(gram_diff * gram_diff) + EPS)
    teacher_norm = jnp.sqrt(total(gram_teacher * gram_teacher))
    loss_out[...] = diff_norm / teacher_norm
    d_gram = LOSS_SCALE * gram_diff / (diff_norm * teacher_norm)
    spread = jnp.dot(
        jnp.concatenate(split3(d_gram), axis=0), embed, preferred_element_type=F32
    )
    d_embed = 2.0 * (spread[:docs] + (spread[docs : 2 * docs] + spread[2 * docs :]))
    along = jnp.sum(unit_rows * d_embed, axis=1, keepdims=True)
    d_all = ((d_embed - unit_rows * along) * inv_norm / count_all).astype(BF16)

    pick = lax.broadcasted_iota(jnp.int32, (16, docs), 0)
    wanted = jnp.where(
        pick < docs_dev, me * docs_dev + pick, sibling * docs_dev + pick - docs_dev
    )
    chosen = (wanted == lax.broadcasted_iota(jnp.int32, (16, docs), 1)).astype(F32).astype(BF16)
    d_pair = jnp.dot(chosen, d_all, preferred_element_type=F32).astype(BF16)
    d_pair_hidden = rows_product(d_pair, w_down[...])
    for c in range(chunks):
        at = (c % pieces) * width
        d_hid[c] = d_pair_hidden[:, at : at + width]

    feats_copy.wait_recv()

    def y_copy(c):
        return pltpu.make_async_remote_copy(
            src_ref=y_send.at[c], dst_ref=y_recv.at[c], send_sem=y_ssem.at[c],
            recv_sem=y_rsem.at[c], device_id={"dp": across}, device_id_type=MESH,
        )

    def z_copy(c, there, src):
        return pltpu.make_async_remote_copy(
            src_ref=z_send.at[c, there], dst_ref=z_recv.at[c, src],
            send_sem=z_ssem.at[c, there], recv_sem=z_rsem.at[c, src],
            device_id={"dp": there * 4 + row * 2 + core}, device_id_type=MESH,
        )

    def col_peer(d):
        return lax.rem(col + d, cols)

    @pl.loop(0, chunks)
    def _(c):
        acts_copy(c).wait_recv()
        d_mine, d_other = [], []
        for d in range(docs_dev):
            token_at = slice(d * seq, (d + 1) * seq)
            mine = d_hid[c, d : d + 1]
            other = d_hid[c, docs_dev + d : docs_dev + d + 1]
            d_mine.append((acts[0, c, token_at].astype(F32) * mine).astype(BF16))
            d_other.append((acts[1, c, token_at].astype(F32) * other).astype(BF16))
        d_mine = jnp.concatenate(d_mine, axis=0)
        d_other = jnp.concatenate(d_other, axis=0)

        def term(side):
            own = feats[:, side, core].reshape(cols * rows, tokens)
            given = feats_in[:, side].reshape(cols * rows, tokens)
            both = jnp.dot(own, d_mine, preferred_element_type=F32) + jnp.dot(
                given, d_other, preferred_element_type=F32
            )
            return both.reshape(cols, rows, width)

        y_send[c] = term(1 - row).astype(BF16)
        y_copy(c).start()
        y_part[c] = term(row)

    own_rows = lax.broadcasted_iota(jnp.int32, (down_rows, hidden_width), 0) + me * down_rows
    select = (
        own_rows == lax.broadcasted_iota(jnp.int32, (down_rows, hidden_width), 1)
    ).astype(F32).astype(BF16)
    own_sums = rows_product(select, sums).astype(BF16)
    down_out[...] = jnp.dot(
        own_sums, jnp.concatenate([d_all] * 3, axis=0), preferred_element_type=F32
    )

    @pl.loop(0, chunks)
    def _(c):
        y_copy(c).wait_recv()
        both = y_part[c] + y_recv[c].astype(F32)
        y_part[c] = both
        z_send[c] = both.astype(BF16)
        z_part[c] = y_part[c, col]

        @pl.loop(1, cols)
        def _(d):
            z_copy(c, col_peer(d), col).start()

    @pl.loop(0, chunks)
    def _(c):
        @pl.loop(1, cols)
        def _(d):
            z_copy(c, col, col_peer(d)).wait_recv()
            z_part[c] += z_recv[c, col_peer(d)].astype(F32)

    for c in range(pieces):
        gate_out[:, c * width : (c + 1) * width] = z_part[c]
        up_out[:, c * width : (c + 1) * width] = z_part[c + pieces]

    feats_copy.wait_send()

    @pl.loop(1, n)
    def _(d):
        t_copy(peer(d), me).wait_send()
        p_copy(peer(d), me).wait_send()
        g_copy(peer(d), me).wait_send()

    @pl.loop(0, chunks)
    def _(c):
        acts_copy(c).wait_send()
        y_copy(c).wait_send()

        @pl.loop(1, cols)
        def _(d):
            z_copy(c, col_peer(d), col).wait_send()


def solution(mesh):
    n = mesh.shape["dp"]
    in_specs = (
        P(("groups", "dp"), None),
        P(("groups", "dp")),
        P(),
        P(),
        P(),
        P(),
        P("groups", "dp"),
        P("dp", None),
        P("groups", None),
        P(),
    )
    out_specs = (
        P("groups"),
        P(("groups", "dp"), None),
        P(("groups", "dp"), None),
        P(("groups", "dp"), None),
    )

    def per_device(
        states, lengths, norm_gain, w_gate, w_up, w_down, context, w_out, resid_stream, teacher_gain
    ):
        tokens, model = states.shape
        hidden_width = w_gate.shape[1]
        docs_dev = lengths.shape[0]
        docs = context.shape[0]
        teacher_width = w_out.shape[1]
        feat = teacher_width // n
        rows = model // n
        width = 512
        chunks = 2 * hidden_width // width
        cols = n // 4
        fold = max(1, 128 // docs)
        packed = hidden_width + model + 128
        vmem = pl.BlockSpec(memory_space=pltpu.VMEM)
        sem = pltpu.SemaphoreType.DMA
        loss, grad_gate, grad_up, grad_down = pl.pallas_call(
            functools.partial(step_kernel, n, width),
            out_shape=(
                jax.ShapeDtypeStruct((1, 1), F32),
                jax.ShapeDtypeStruct((rows, hidden_width), F32),
                jax.ShapeDtypeStruct((rows, hidden_width), F32),
                jax.ShapeDtypeStruct((hidden_width // n, model), F32),
            ),
            in_specs=[vmem, pl.BlockSpec(memory_space=pltpu.SMEM)] + [vmem] * 8,
            out_specs=(vmem,) * 4,
            scratch_shapes=[
                pltpu.VMEM((n, docs, feat), BF16),
                pltpu.VMEM((n, docs, feat), BF16),
                pltpu.VMEM((n, docs // fold, docs * fold), F32),
                pltpu.VMEM((n, docs_dev, packed), F32),
                pltpu.VMEM((docs, packed), F32),
                pltpu.VMEM((cols, 2, 2, rows, tokens), BF16),
                pltpu.VMEM((cols, 2, rows, tokens), BF16),
                pltpu.VMEM((2, chunks, tokens, width), BF16),
                pltpu.VMEM((chunks, 16, width), F32),
                pltpu.VMEM((chunks, cols, rows, width), BF16),
                pltpu.VMEM((chunks, cols, rows, width), F32),
                pltpu.VMEM((chunks, cols, rows, width), BF16),
                pltpu.VMEM((chunks, cols, rows, width), BF16),
                pltpu.VMEM((chunks, cols, rows, width), BF16),
                pltpu.VMEM((chunks, rows, width), F32),
                sem((n,)), sem((n,)), sem((n,)), sem((n,)), sem((n,)), sem((n,)),
                sem((chunks + 1,)), sem((chunks + 1,)),
                sem((chunks,)), sem((chunks,)),
                sem((chunks, cols)), sem((chunks, cols)),
            ],
            compiler_params=pltpu.CompilerParams(
                collective_id=0, has_side_effects=True, vmem_limit_bytes=60 * 1024 * 1024
            ),
        )(
            states, lengths, norm_gain.reshape(1, -1), w_gate, w_up, w_down, context, w_out,
            resid_stream, teacher_gain.reshape(1, -1),
        )
        return (loss.reshape(1), grad_gate, grad_up, grad_down)

    return jax.shard_map(
        per_device, mesh=mesh, in_specs=in_specs, out_specs=out_specs, check_vma=False
    )
```

```python
import functools

import jax
import jax.numpy as jnp
from jax import lax
from jax.experimental import pallas as pl
from jax.experimental.pallas import tpu as pltpu
from jax.sharding import PartitionSpec as P

EPS = 1e-06
LOSS_SCALE = 4096.0
MESH = pl.DeviceIdType.MESH
F32 = jnp.float32
BF16 = jnp.bfloat16


def rows_product(left_rows, right_rows):
    return lax.dot_general(
        left_rows, right_rows, (((1,), (1,)), ((), ())), preferred_element_type=F32
    )


def split3(wide):
    high = wide.astype(BF16)
    rest = wide - high.astype(F32)
    middle = rest.astype(BF16)
    low = (rest - middle.astype(F32)).astype(BF16)
    return high, middle, low


def step_kernel(
    n, width,
    states_in, lengths, norm_gain, w_gate_in, w_up_in, w_down_in, context_in, w_out_in, resid_in, gain,
    loss_out, gate_out, up_out, down_out,
    states, w_gate, w_up, w_down, context, w_out, resid,
    t_send, t_recv, g_all, p_all, h_all, s_own, big, big_h, feats, feats_in, acts, d_hid,
    y_send, y_part, y_recv, z_send, z_recv, z_part,
    in_sem, wide_sem, t_ssem, t_rsem, g_ssem, g_rsem, p_ssem, p_rsem, h_ssem, h_rsem, s_ssem, s_rsem,
    y_ssem, y_rsem, z_ssem, z_rsem,
):
    me = lax.axis_index("dp")
    core = lax.rem(me, 2)
    row = lax.rem(lax.div(me, 2), 2)
    col = lax.div(me, 4)
    cols = n // 4
    sibling = me + 1 - 2 * core
    across = me + 2 - 4 * row
    docs_dev = lengths.shape[0]
    tokens, model = states.shape
    seq = tokens // docs_dev
    hidden_width = w_gate.shape[1]
    docs = context.shape[0]
    feat = w_out.shape[1] // n
    rows = model // n
    down_rows = hidden_width // n
    pieces = hidden_width // width
    chunks = 2 * pieces

    def peer(d):
        return lax.rem(me + d, n)

    def load(i, src, dst):
        copy = pltpu.make_async_copy(src, dst, in_sem.at[i])
        copy.start()
        return copy

    def load_wide(c):
        at = pl.ds(pl.multiple_of(c * width, width), width)
        return (
            pltpu.make_async_copy(w_gate_in.at[:, at], w_gate.at[:, at], wide_sem.at[0, c]),
            pltpu.make_async_copy(w_up_in.at[:, at], w_up.at[:, at], wide_sem.at[1, c]),
        )

    context_load = load(0, context_in, context)
    w_out_load = load(1, w_out_in, w_out)
    resid_load = load(2, resid_in, resid)
    states_load = load(3, states_in, states)
    for c in range(pieces):
        for copy in load_wide(c):
            copy.start()
    w_down_load = load(4, w_down_in, w_down)

    barrier = pltpu.get_barrier_semaphore()

    @pl.loop(1, n)
    def _(d):
        pl.semaphore_signal(barrier, inc=1, device_id={"dp": peer(d)}, device_id_type=MESH)

    context_load.wait()
    w_out_load.wait()
    resid_load.wait()
    partial = jnp.dot(context[...], w_out[...], preferred_element_type=F32)
    first = (me == 0).astype(F32)
    partial = gain[...].astype(F32).reshape(1, -1) * (partial + first * resid[...].astype(F32))
    for j in range(n):
        t_send[j] = partial[:, j * feat : (j + 1) * feat].astype(BF16)
    t_recv[me] = t_send[me]
    pl.semaphore_wait(barrier, n - 1)

    def t_copy(dst, src):
        return pltpu.make_async_remote_copy(
            src_ref=t_send.at[dst], dst_ref=t_recv.at[src], send_sem=t_ssem.at[dst],
            recv_sem=t_rsem.at[src], device_id={"dp": dst}, device_id_type=MESH,
        )

    @pl.loop(1, n)
    def _(d):
        t_copy(peer(d), me).start()

    states_load.wait()
    normed_parts = []
    masks = []
    for d in range(docs_dev):
        x = states[d * seq : (d + 1) * seq].astype(F32)
        inv_rms = lax.rsqrt(jnp.mean(x * x, axis=1, keepdims=True) + EPS)
        normed_wide = x * inv_rms * norm_gain[...].astype(F32).reshape(1, -1)
        normed = normed_wide.astype(BF16)
        normed_parts.append(normed)
        turned = normed.astype(F32).T.astype(BF16)
        feats[:, :, :, :, d * seq : (d + 1) * seq] = turned.reshape(cols, 2, 2, rows, seq)
        length = lengths[d]
        mask = (lax.broadcasted_iota(jnp.int32, (seq, 1), 0) < length).astype(F32)
        masks.append(mask)
        s_own[d : d + 1] = jnp.sum(x * mask, axis=0, keepdims=True)
        p_all[me, d : d + 1, model:] = jnp.zeros((1, 128), F32) + length.astype(F32)
    normed = jnp.concatenate(normed_parts, axis=0)
    mask = jnp.concatenate(masks, axis=0)

    feats_copy = pltpu.make_async_remote_copy(
        src_ref=feats.at[:, :, 1 - core], dst_ref=feats_in, send_sem=s_ssem.at[chunks],
        recv_sem=s_rsem.at[chunks], device_id={"dp": sibling}, device_id_type=MESH,
    )
    feats_copy.start()

    def acts_copy(c):
        return pltpu.make_async_remote_copy(
            src_ref=acts.at[0, c], dst_ref=acts.at[1, c], send_sem=s_ssem.at[c],
            recv_sem=s_rsem.at[c], device_id={"dp": sibling}, device_id_type=MESH,
        )

    @pl.loop(0, pieces)
    def _(c):
        at = pl.ds(pl.multiple_of(c * width, width), width)
        for copy in load_wide(c):
            copy.wait()
        gate_pre = jnp.dot(normed, w_gate[:, at], preferred_element_type=F32)
        up_pre = jnp.dot(normed, w_up[:, at], preferred_element_type=F32)
        sig = jax.nn.sigmoid(gate_pre)
        silu = gate_pre * sig
        hidden = (silu * up_pre).astype(BF16).astype(F32) * mask
        for d in range(docs_dev):
            h_all[me, d : d + 1, at] = jnp.sum(
                hidden[d * seq : (d + 1) * seq], axis=0, keepdims=True
            )
        acts[0, c] = (mask * up_pre * sig * (1.0 + gate_pre * (1.0 - sig))).astype(BF16)
        acts[0, c + pieces] = (mask * silu).astype(BF16)

    def p_copy(dst, src):
        return pltpu.make_async_remote_copy(
            src_ref=p_all.at[src], dst_ref=p_all.at[src], send_sem=p_ssem.at[dst],
            recv_sem=p_rsem.at[src], device_id={"dp": dst}, device_id_type=MESH,
        )

    def h_copy(dst, src):
        return pltpu.make_async_remote_copy(
            src_ref=h_all.at[src], dst_ref=h_all.at[src], send_sem=h_ssem.at[dst],
            recv_sem=h_rsem.at[src], device_id={"dp": dst}, device_id_type=MESH,
        )

    def g_copy(dst, src):
        return pltpu.make_async_remote_copy(
            src_ref=g_all.at[src], dst_ref=g_all.at[src], send_sem=g_ssem.at[dst],
            recv_sem=g_rsem.at[src], device_id={"dp": dst}, device_id_type=MESH,
        )

    w_down_load.wait()
    own_parts = jnp.concatenate([part.astype(F32) for part in split3(h_all[me])], axis=0)
    lifted = jnp.dot(own_parts.astype(BF16), w_down[...], preferred_element_type=F32)
    lifted = lifted[:docs_dev] + (lifted[docs_dev : 2 * docs_dev] + lifted[2 * docs_dev :])
    p_all[me, :, :model] = (s_own[...] + lifted) / p_all[me, :, model : model + 1]

    @pl.loop(1, n)
    def _(d):
        p_copy(peer(d), me).start()

    @pl.loop(1, n)
    def _(d):
        t_copy(me, peer(d)).wait_recv()

    scaled = jnp.sum(t_recv[...].astype(F32), axis=0)
    gram_part = lax.dot_general(
        scaled, scaled, (((1,), (1,)), ((), ())), precision=lax.Precision.HIGHEST,
        preferred_element_type=F32,
    )
    fold = max(1, 128 // docs)
    fold_rows = docs // fold
    g_all[me] = jnp.concatenate(
        [gram_part[i * fold_rows : (i + 1) * fold_rows] for i in range(fold)], axis=1
    )

    @pl.loop(1, n)
    def _(d):
        g_copy(peer(d), me).start()

    @pl.loop(1, n)
    def _(d):
        h_copy(peer(d), me).start()

    @pl.loop(0, chunks)
    def _(c):
        acts_copy(c).start()

    @pl.loop(1, n)
    def _(d):
        p_copy(me, peer(d)).wait_recv()

    for j in range(n):
        big[j * docs_dev : (j + 1) * docs_dev, :] = p_all[j]
    count_all = big[:, model : model + 1]
    pooled = big[:, :model]
    inv_norm = lax.rsqrt(jnp.sum(pooled * pooled, axis=1, keepdims=True) + EPS)
    unit_rows = pooled * inv_norm
    embed = unit_rows.astype(BF16)
    gram_student = rows_product(embed, embed)

    @pl.loop(1, n)
    def _(d):
        g_copy(me, peer(d)).wait_recv()

    folded = jnp.sum(g_all[...], axis=0)
    gram_raw = jnp.concatenate(
        [folded[:, i * docs : (i + 1) * docs] for i in range(fold)], axis=0
    )
    diagonal = lax.broadcasted_iota(jnp.int32, (docs, docs), 0) == lax.broadcasted_iota(
        jnp.int32, (docs, docs), 1
    )
    squares = jnp.where(diagonal, gram_raw, 0.0)
    inv_col = lax.rsqrt(jnp.sum(squares, axis=1, keepdims=True) + EPS)
    inv_row = lax.rsqrt(jnp.sum(squares, axis=0, keepdims=True) + EPS)
    gram_teacher = gram_raw * inv_col * inv_row
    gram_diff = gram_student - gram_teacher

    def total(square):
        return jnp.sum(jnp.sum(square, axis=1, keepdims=True), axis=0, keepdims=True)

    diff_norm = jnp.sqrt(total(gram_diff * gram_diff) + EPS)
    teacher_norm = jnp.sqrt(total(gram_teacher * gram_teacher))
    loss_out[...] = diff_norm / teacher_norm
    d_gram = LOSS_SCALE * gram_diff / (diff_norm * teacher_norm)
    spread = jnp.dot(
        jnp.concatenate(split3(d_gram), axis=0), embed, preferred_element_type=F32
    )
    d_embed = 2.0 * (spread[:docs] + (spread[docs : 2 * docs] + spread[2 * docs :]))
    along = jnp.sum(unit_rows * d_embed, axis=1, keepdims=True)
    d_all = ((d_embed - unit_rows * along) * inv_norm / count_all).astype(BF16)

    pick = lax.broadcasted_iota(jnp.int32, (16, docs), 0)
    wanted = jnp.where(
        pick < docs_dev, me * docs_dev + pick, sibling * docs_dev + pick - docs_dev
    )
    chosen = (wanted == lax.broadcasted_iota(jnp.int32, (16, docs), 1)).astype(F32).astype(BF16)
    d_pair = jnp.dot(chosen, d_all, preferred_element_type=F32).astype(BF16)
    d_pair_hidden = rows_product(d_pair, w_down[...])
    for c in range(chunks):
        at = (c % pieces) * width
        d_hid[c] = d_pair_hidden[:, at : at + width]

    feats_copy.wait_recv()

    def y_copy(c):
        return pltpu.make_async_remote_copy(
            src_ref=y_send.at[c], dst_ref=y_recv.at[c], send_sem=y_ssem.at[c],
            recv_sem=y_rsem.at[c], device_id={"dp": across}, device_id_type=MESH,
        )

    def z_copy(c, there, src):
        return pltpu.make_async_remote_copy(
            src_ref=z_send.at[c, there], dst_ref=z_recv.at[c, src],
            send_sem=z_ssem.at[c, there], recv_sem=z_rsem.at[c, src],
            device_id={"dp": there * 4 + row * 2 + core}, device_id_type=MESH,
        )

    def col_peer(d):
        return lax.rem(col + d, cols)

    @pl.loop(0, chunks)
    def _(c):
        acts_copy(c).wait_recv()
        d_mine, d_other = [], []
        for d in range(docs_dev):
            token_at = slice(d * seq, (d + 1) * seq)
            mine = d_hid[c, d : d + 1]
            other = d_hid[c, docs_dev + d : docs_dev + d + 1]
            d_mine.append((acts[0, c, token_at].astype(F32) * mine).astype(BF16))
            d_other.append((acts[1, c, token_at].astype(F32) * other).astype(BF16))
        d_mine = jnp.concatenate(d_mine, axis=0)
        d_other = jnp.concatenate(d_other, axis=0)

        def term(side):
            own = feats[:, side, core].reshape(cols * rows, tokens)
            given = feats_in[:, side].reshape(cols * rows, tokens)
            both = jnp.dot(own, d_mine, preferred_element_type=F32) + jnp.dot(
                given, d_other, preferred_element_type=F32
            )
            return both.reshape(cols, rows, width)

        y_send[c] = term(1 - row).astype(BF16)
        y_copy(c).start()
        y_part[c] = term(row)

    @pl.loop(1, n)
    def _(d):
        h_copy(me, peer(d)).wait_recv()

    for j in range(n):
        big_h[j * docs_dev : (j + 1) * docs_dev, :] = h_all[j]
    sums = jnp.concatenate(split3(big_h[...]), axis=0)
    own_rows = lax.broadcasted_iota(jnp.int32, (down_rows, hidden_width), 0) + me * down_rows
    select = (
        own_rows == lax.broadcasted_iota(jnp.int32, (down_rows, hidden_width), 1)
    ).astype(F32).astype(BF16)
    own_sums = rows_product(select, sums).astype(BF16)
    down_out[...] = jnp.dot(
        own_sums, jnp.concatenate([d_all] * 3, axis=0), preferred_element_type=F32
    )

    @pl.loop(0, chunks)
    def _(c):
        y_copy(c).wait_recv()
        both = y_part[c] + y_recv[c].astype(F32)
        y_part[c] = both
        z_send[c] = both.astype(BF16)
        z_part[c] = y_part[c, col]

        @pl.loop(1, cols)
        def _(d):
            z_copy(c, col_peer(d), col).start()

    @pl.loop(0, chunks)
    def _(c):
        @pl.loop(1, cols)
        def _(d):
            z_copy(c, col, col_peer(d)).wait_recv()
            z_part[c] += z_recv[c, col_peer(d)].astype(F32)

    for c in range(pieces):
        gate_out[:, c * width : (c + 1) * width] = z_part[c]
        up_out[:, c * width : (c + 1) * width] = z_part[c + pieces]

    feats_copy.wait_send()

    @pl.loop(1, n)
    def _(d):
        t_copy(peer(d), me).wait_send()
        p_copy(peer(d), me).wait_send()
        g_copy(peer(d), me).wait_send()
        h_copy(peer(d), me).wait_send()

    @pl.loop(0, chunks)
    def _(c):
        acts_copy(c).wait_send()
        y_copy(c).wait_send()

        @pl.loop(1, cols)
        def _(d):
            z_copy(c, col_peer(d), col).wait_send()


def hand_over(gate, up, down, gate_out, up_out, down_out):
    gate_out[...] = gate[...]
    up_out[...] = up[...]
    down_out[...] = down[...]


def solution(mesh):
    n = mesh.shape["dp"]
    in_specs = (
        P(("groups", "dp"), None),
        P(("groups", "dp")),
        P(),
        P(),
        P(),
        P(),
        P("groups", "dp"),
        P("dp", None),
        P("groups", None),
        P(),
    )
    out_specs = (
        P("groups"),
        P(("groups", "dp"), None),
        P(("groups", "dp"), None),
        P(("groups", "dp"), None),
    )

    def per_device(
        states, lengths, norm_gain, w_gate, w_up, w_down, context, w_out, resid_stream, teacher_gain
    ):
        tokens, model = states.shape
        hidden_width = w_gate.shape[1]
        docs_dev = lengths.shape[0]
        docs = context.shape[0]
        teacher_width = w_out.shape[1]
        feat = teacher_width // n
        rows = model // n
        width = 256
        chunks = 2 * hidden_width // width
        cols = n // 4
        fold = max(1, 128 // docs)
        packed = model + 128
        hbm = pl.BlockSpec(memory_space=pl.ANY)
        vmem = pl.BlockSpec(memory_space=pltpu.VMEM)
        sem = pltpu.SemaphoreType.DMA
        loss, grad_gate, grad_up, grad_down = pl.pallas_call(
            functools.partial(step_kernel, n, width),
            out_shape=(
                jax.ShapeDtypeStruct((1, 1), F32),
                jax.ShapeDtypeStruct((rows, hidden_width), F32),
                jax.ShapeDtypeStruct((rows, hidden_width), F32),
                jax.ShapeDtypeStruct((hidden_width // n, model), F32),
            ),
            in_specs=[hbm, pl.BlockSpec(memory_space=pltpu.SMEM), vmem] + [hbm] * 6 + [vmem],
            out_specs=(vmem,) * 4,
            scratch_shapes=[
                pltpu.VMEM((tokens, model), BF16),
                pltpu.VMEM((model, hidden_width), BF16),
                pltpu.VMEM((model, hidden_width), BF16),
                pltpu.VMEM((hidden_width, model), BF16),
                pltpu.VMEM(context.shape, BF16),
                pltpu.VMEM(w_out.shape, BF16),
                pltpu.VMEM(resid_stream.shape, BF16),
                pltpu.VMEM((n, docs, feat), BF16),
                pltpu.VMEM((n, docs, feat), BF16),
                pltpu.VMEM((n, docs // fold, docs * fold), F32),
                pltpu.VMEM((n, docs_dev, packed), F32),
                pltpu.VMEM((n, docs_dev, hidden_width), F32),
                pltpu.VMEM((docs_dev, model), F32),
                pltpu.VMEM((docs, packed), F32),
                pltpu.VMEM((docs, hidden_width), F32),
                pltpu.VMEM((cols, 2, 2, rows, tokens), BF16),
                pltpu.VMEM((cols, 2, rows, tokens), BF16),
                pltpu.VMEM((2, chunks, tokens, width), BF16),
                pltpu.VMEM((chunks, 16, width), F32),
                pltpu.VMEM((chunks, cols, rows, width), BF16),
                pltpu.VMEM((chunks, cols, rows, width), F32),
                pltpu.VMEM((chunks, cols, rows, width), BF16),
                pltpu.VMEM((chunks, cols, rows, width), BF16),
                pltpu.VMEM((chunks, cols, rows, width), BF16),
                pltpu.VMEM((chunks, rows, width), F32),
                sem((5,)), sem((2, chunks // 2)),
                sem((n,)), sem((n,)), sem((n,)), sem((n,)), sem((n,)), sem((n,)), sem((n,)), sem((n,)),
                sem((chunks + 1,)), sem((chunks + 1,)),
                sem((chunks,)), sem((chunks,)),
                sem((chunks, cols)), sem((chunks, cols)),
            ],
            compiler_params=pltpu.CompilerParams(
                collective_id=0, has_side_effects=True, vmem_limit_bytes=60 * 1024 * 1024
            ),
        )(
            states, lengths, norm_gain, w_gate, w_up, w_down, context, w_out,
            resid_stream, teacher_gain,
        )
        made = (grad_gate, grad_up, grad_down)
        made = pl.pallas_call(
            hand_over,
            out_shape=tuple(jax.ShapeDtypeStruct(g.shape, g.dtype) for g in made),
            in_specs=[vmem] * 3,
            out_specs=(vmem,) * 3,
        )(*made)
        return (loss.reshape(1), *made)

    return jax.shard_map(
        per_device, mesh=mesh, in_specs=in_specs, out_specs=out_specs, check_vma=False
    )
```

```python
import functools

import jax
import jax.numpy as jnp
from jax import lax
from jax.experimental import pallas as pl
from jax.experimental.pallas import tpu as pltpu
from jax.sharding import PartitionSpec as P

EPS = 1e-06
LOSS_SCALE = 4096.0
MESH = pl.DeviceIdType.MESH
F32 = jnp.float32
BF16 = jnp.bfloat16


def rows_product(left_rows, right_rows):
    return lax.dot_general(
        left_rows, right_rows, (((1,), (1,)), ((), ())), preferred_element_type=F32
    )


def split3(wide):
    high = wide.astype(BF16)
    rest = wide - high.astype(F32)
    middle = rest.astype(BF16)
    low = (rest - middle.astype(F32)).astype(BF16)
    return high, middle, low


def step_kernel(
    n, width,
    states_in, lengths, norm_gain, w_gate_in, w_up_in, w_down_in, context_in, w_out_in, resid_in, gain,
    loss_out, gate_out, up_out, down_out,
    states, w_gate, w_up, w_down, context, w_out, resid,
    t_send, t_recv, g_all, p_all, h_all, s_own, big, big_h, feats, feats_in, acts, d_hid,
    y_send, y_part, y_recv, n_send, n_recv, z_send, z_recv, z_part,
    in_sem, wide_sem, t_ssem, t_rsem, g_ssem, g_rsem, p_ssem, p_rsem, h_ssem, h_rsem, s_ssem, s_rsem,
    y_ssem, y_rsem, n_ssem, n_rsem, z_ssem, z_rsem,
):
    me = lax.axis_index("dp")
    core = lax.rem(me, 2)
    row = lax.rem(lax.div(me, 2), 2)
    col = lax.div(me, 4)
    cols = n // 4
    sibling = me + 1 - 2 * core
    across = me + 2 - 4 * row
    docs_dev = lengths.shape[0]
    tokens, model = states.shape
    seq = tokens // docs_dev
    hidden_width = w_gate.shape[1]
    docs = context.shape[0]
    feat = w_out.shape[1] // n
    rows = model // n
    down_rows = hidden_width // n
    pieces = hidden_width // width
    chunks = 2 * pieces

    def peer(d):
        return lax.rem(me + d, n)

    def load(i, src, dst):
        copy = pltpu.make_async_copy(src, dst, in_sem.at[i])
        copy.start()
        return copy

    def load_wide(c):
        at = pl.ds(pl.multiple_of(c * width, width), width)
        return (
            pltpu.make_async_copy(w_gate_in.at[:, at], w_gate.at[:, at], wide_sem.at[0, c]),
            pltpu.make_async_copy(w_up_in.at[:, at], w_up.at[:, at], wide_sem.at[1, c]),
        )

    context_load = load(0, context_in, context)
    w_out_load = load(1, w_out_in, w_out)
    resid_load = load(2, resid_in, resid)
    states_load = load(3, states_in, states)
    for c in range(pieces):
        for copy in load_wide(c):
            copy.start()
    w_down_load = load(4, w_down_in, w_down)

    barrier = pltpu.get_barrier_semaphore()

    @pl.loop(1, n)
    def _(d):
        pl.semaphore_signal(barrier, inc=1, device_id={"dp": peer(d)}, device_id_type=MESH)

    context_load.wait()
    w_out_load.wait()
    resid_load.wait()
    partial = jnp.dot(context[...], w_out[...], preferred_element_type=F32)
    first = (me == 0).astype(F32)
    partial = gain[...].astype(F32).reshape(1, -1) * (partial + first * resid[...].astype(F32))
    for j in range(n):
        t_send[j] = partial[:, j * feat : (j + 1) * feat].astype(BF16)
    t_recv[me] = t_send[me]
    pl.semaphore_wait(barrier, n - 1)

    def t_copy(dst, src):
        return pltpu.make_async_remote_copy(
            src_ref=t_send.at[dst], dst_ref=t_recv.at[src], send_sem=t_ssem.at[dst],
            recv_sem=t_rsem.at[src], device_id={"dp": dst}, device_id_type=MESH,
        )

    @pl.loop(1, n)
    def _(d):
        t_copy(peer(d), me).start()

    states_load.wait()
    normed_parts = []
    masks = []
    for d in range(docs_dev):
        x = states[d * seq : (d + 1) * seq].astype(F32)
        inv_rms = lax.rsqrt(jnp.mean(x * x, axis=1, keepdims=True) + EPS)
        normed_wide = x * inv_rms * norm_gain[...].astype(F32).reshape(1, -1)
        normed = normed_wide.astype(BF16)
        normed_parts.append(normed)
        turned = normed.astype(F32).T.astype(BF16)
        feats[:, :, :, :, d * seq : (d + 1) * seq] = turned.reshape(cols, 2, 2, rows, seq)
        length = lengths[d]
        mask = (lax.broadcasted_iota(jnp.int32, (seq, 1), 0) < length).astype(F32)
        masks.append(mask)
        s_own[d : d + 1] = jnp.sum(x * mask, axis=0, keepdims=True)
        p_all[me, d : d + 1, model:] = jnp.zeros((1, 128), F32) + length.astype(F32)
    normed = jnp.concatenate(normed_parts, axis=0)
    mask = jnp.concatenate(masks, axis=0)

    feats_copy = pltpu.make_async_remote_copy(
        src_ref=feats.at[:, :, 1 - core], dst_ref=feats_in, send_sem=s_ssem.at[chunks],
        recv_sem=s_rsem.at[chunks], device_id={"dp": sibling}, device_id_type=MESH,
    )
    feats_copy.start()

    def acts_copy(c):
        return pltpu.make_async_remote_copy(
            src_ref=acts.at[0, c], dst_ref=acts.at[1, c], send_sem=s_ssem.at[c],
            recv_sem=s_rsem.at[c], device_id={"dp": sibling}, device_id_type=MESH,
        )

    @pl.loop(0, pieces)
    def _(c):
        at = pl.ds(pl.multiple_of(c * width, width), width)
        for copy in load_wide(c):
            copy.wait()
        gate_pre = jnp.dot(normed, w_gate[:, at], preferred_element_type=F32)
        up_pre = jnp.dot(normed, w_up[:, at], preferred_element_type=F32)
        sig = jax.nn.sigmoid(gate_pre)
        silu = gate_pre * sig
        hidden = (silu * up_pre).astype(BF16).astype(F32) * mask
        for d in range(docs_dev):
            h_all[me, d : d + 1, at] = jnp.sum(
                hidden[d * seq : (d + 1) * seq], axis=0, keepdims=True
            )
        acts[0, c] = (mask * up_pre * sig * (1.0 + gate_pre * (1.0 - sig))).astype(BF16)
        acts[0, c + pieces] = (mask * silu).astype(BF16)

    def p_copy(dst, src):
        return pltpu.make_async_remote_copy(
            src_ref=p_all.at[src], dst_ref=p_all.at[src], send_sem=p_ssem.at[dst],
            recv_sem=p_rsem.at[src], device_id={"dp": dst}, device_id_type=MESH,
        )

    def h_copy(dst, src):
        return pltpu.make_async_remote_copy(
            src_ref=h_all.at[src], dst_ref=h_all.at[src], send_sem=h_ssem.at[dst],
            recv_sem=h_rsem.at[src], device_id={"dp": dst}, device_id_type=MESH,
        )

    def g_copy(dst, src):
        return pltpu.make_async_remote_copy(
            src_ref=g_all.at[src], dst_ref=g_all.at[src], send_sem=g_ssem.at[dst],
            recv_sem=g_rsem.at[src], device_id={"dp": dst}, device_id_type=MESH,
        )

    w_down_load.wait()
    own_parts = jnp.concatenate([part.astype(F32) for part in split3(h_all[me])], axis=0)
    lifted = jnp.dot(own_parts.astype(BF16), w_down[...], preferred_element_type=F32)
    lifted = lifted[:docs_dev] + (lifted[docs_dev : 2 * docs_dev] + lifted[2 * docs_dev :])
    p_all[me, :, :model] = (s_own[...] + lifted) / p_all[me, :, model : model + 1]

    @pl.loop(1, n)
    def _(d):
        p_copy(peer(d), me).start()

    @pl.loop(1, n)
    def _(d):
        t_copy(me, peer(d)).wait_recv()

    scaled = jnp.sum(t_recv[...].astype(F32), axis=0)
    gram_part = lax.dot_general(
        scaled, scaled, (((1,), (1,)), ((), ())), precision=lax.Precision.HIGHEST,
        preferred_element_type=F32,
    )
    fold = max(1, 128 // docs)
    fold_rows = docs // fold
    g_all[me] = jnp.concatenate(
        [gram_part[i * fold_rows : (i + 1) * fold_rows] for i in range(fold)], axis=1
    )

    @pl.loop(1, n)
    def _(d):
        g_copy(peer(d), me).start()

    @pl.loop(1, n)
    def _(d):
        h_copy(peer(d), me).start()

    @pl.loop(0, chunks)
    def _(c):
        acts_copy(c).start()

    @pl.loop(1, n)
    def _(d):
        p_copy(me, peer(d)).wait_recv()

    for j in range(n):
        big[j * docs_dev : (j + 1) * docs_dev, :] = p_all[j]
    count_all = big[:, model : model + 1]
    pooled = big[:, :model]
    inv_norm = lax.rsqrt(jnp.sum(pooled * pooled, axis=1, keepdims=True) + EPS)
    unit_rows = pooled * inv_norm
    embed = unit_rows.astype(BF16)
    gram_student = rows_product(embed, embed)

    @pl.loop(1, n)
    def _(d):
        g_copy(me, peer(d)).wait_recv()

    folded = jnp.sum(g_all[...], axis=0)
    gram_raw = jnp.concatenate(
        [folded[:, i * docs : (i + 1) * docs] for i in range(fold)], axis=0
    )
    diagonal = lax.broadcasted_iota(jnp.int32, (docs, docs), 0) == lax.broadcasted_iota(
        jnp.int32, (docs, docs), 1
    )
    squares = jnp.where(diagonal, gram_raw, 0.0)
    inv_col = lax.rsqrt(jnp.sum(squares, axis=1, keepdims=True) + EPS)
    inv_row = lax.rsqrt(jnp.sum(squares, axis=0, keepdims=True) + EPS)
    gram_teacher = gram_raw * inv_col * inv_row
    gram_diff = gram_student - gram_teacher

    def total(square):
        return jnp.sum(jnp.sum(square, axis=1, keepdims=True), axis=0, keepdims=True)

    diff_norm = jnp.sqrt(total(gram_diff * gram_diff) + EPS)
    teacher_norm = jnp.sqrt(total(gram_teacher * gram_teacher))
    loss_out[...] = diff_norm / teacher_norm
    d_gram = LOSS_SCALE * gram_diff / (diff_norm * teacher_norm)
    spread = jnp.dot(
        jnp.concatenate(split3(d_gram), axis=0), embed, preferred_element_type=F32
    )
    d_embed = 2.0 * (spread[:docs] + (spread[docs : 2 * docs] + spread[2 * docs :]))
    along = jnp.sum(unit_rows * d_embed, axis=1, keepdims=True)
    d_all = ((d_embed - unit_rows * along) * inv_norm / count_all).astype(BF16)

    pick = lax.broadcasted_iota(jnp.int32, (16, docs), 0)
    wanted = jnp.where(
        pick < docs_dev, me * docs_dev + pick, sibling * docs_dev + pick - docs_dev
    )
    chosen = (wanted == lax.broadcasted_iota(jnp.int32, (16, docs), 1)).astype(F32).astype(BF16)
    d_pair = jnp.dot(chosen, d_all, preferred_element_type=F32).astype(BF16)
    d_pair_hidden = rows_product(d_pair, w_down[...])
    for c in range(chunks):
        at = (c % pieces) * width
        d_hid[c] = d_pair_hidden[:, at : at + width]

    feats_copy.wait_recv()

    def y_copy(c):
        return pltpu.make_async_remote_copy(
            src_ref=y_send.at[c], dst_ref=y_recv.at[c], send_sem=y_ssem.at[c],
            recv_sem=y_rsem.at[c], device_id={"dp": across}, device_id_type=MESH,
        )

    parity = lax.rem(col, 2)
    half = lax.div(col, 2)
    halves = cols // 2
    lane = row * 2 + core

    def n_copy(c):
        return pltpu.make_async_remote_copy(
            src_ref=n_send.at[c], dst_ref=n_recv.at[c], send_sem=n_ssem.at[c],
            recv_sem=n_rsem.at[c], device_id={"dp": (col + 1 - 2 * parity) * 4 + lane},
            device_id_type=MESH,
        )

    def z_copy(c, there, src):
        return pltpu.make_async_remote_copy(
            src_ref=z_send.at[c, there], dst_ref=z_recv.at[c, src],
            send_sem=z_ssem.at[c, there], recv_sem=z_rsem.at[c, src],
            device_id={"dp": (there * 2 + parity) * 4 + lane}, device_id_type=MESH,
        )

    def half_peer(d):
        return lax.rem(half + d, halves)

    @pl.loop(0, chunks)
    def _(c):
        acts_copy(c).wait_recv()
        d_mine, d_other = [], []
        for d in range(docs_dev):
            token_at = slice(d * seq, (d + 1) * seq)
            mine = d_hid[c, d : d + 1]
            other = d_hid[c, docs_dev + d : docs_dev + d + 1]
            d_mine.append((acts[0, c, token_at].astype(F32) * mine).astype(BF16))
            d_other.append((acts[1, c, token_at].astype(F32) * other).astype(BF16))
        d_mine = jnp.concatenate(d_mine, axis=0)
        d_other = jnp.concatenate(d_other, axis=0)

        def term(side):
            own = feats[:, side, core].reshape(cols * rows, tokens)
            given = feats_in[:, side].reshape(cols * rows, tokens)
            both = jnp.dot(own, d_mine, preferred_element_type=F32) + jnp.dot(
                given, d_other, preferred_element_type=F32
            )
            return both.reshape(cols // 2, 2, rows, width)

        y_send[c] = term(1 - row).astype(BF16)
        y_copy(c).start()
        y_part[c] = term(row)

    @pl.loop(1, n)
    def _(d):
        h_copy(me, peer(d)).wait_recv()

    for j in range(n):
        big_h[j * docs_dev : (j + 1) * docs_dev, :] = h_all[j]
    sums = jnp.concatenate(split3(big_h[...]), axis=0)
    own_rows = lax.broadcasted_iota(jnp.int32, (down_rows, hidden_width), 0) + me * down_rows
    select = (
        own_rows == lax.broadcasted_iota(jnp.int32, (down_rows, hidden_width), 1)
    ).astype(F32).astype(BF16)
    own_sums = rows_product(select, sums).astype(BF16)
    down_out[...] = jnp.dot(
        own_sums, jnp.concatenate([d_all] * 3, axis=0), preferred_element_type=F32
    )

    def far(c):
        n_copy(c).wait_recv()
        z_send[c] = (y_part[c, :, parity] + n_recv[c].astype(F32)).astype(BF16)
        z_part[c] = y_part[c, half, parity] + n_recv[c, half].astype(F32)

        @pl.loop(1, halves)
        def _(d):
            z_copy(c, half_peer(d), half).start()

    @pl.loop(0, chunks)
    def _(c):
        y_copy(c).wait_recv()
        y_part[c] += y_recv[c].astype(F32)
        n_send[c] = y_part[c, :, 1 - parity].astype(BF16)
        n_copy(c).start()

        @pl.when(c > 0)
        def _():
            far(c - 1)

    far(chunks - 1)

    @pl.loop(0, chunks)
    def _(c):
        @pl.loop(1, halves)
        def _(d):
            z_copy(c, half, half_peer(d)).wait_recv()
            z_part[c] += z_recv[c, half_peer(d)].astype(F32)

    for c in range(pieces):
        gate_out[:, c * width : (c + 1) * width] = z_part[c]
        up_out[:, c * width : (c + 1) * width] = z_part[c + pieces]

    feats_copy.wait_send()

    @pl.loop(1, n)
    def _(d):
        t_copy(peer(d), me).wait_send()
        p_copy(peer(d), me).wait_send()
        g_copy(peer(d), me).wait_send()
        h_copy(peer(d), me).wait_send()

    @pl.loop(0, chunks)
    def _(c):
        acts_copy(c).wait_send()
        y_copy(c).wait_send()
        n_copy(c).wait_send()

        @pl.loop(1, halves)
        def _(d):
            z_copy(c, half_peer(d), half).wait_send()


def hand_over(gate, up, down, gate_out, up_out, down_out):
    gate_out[...] = gate[...]
    up_out[...] = up[...]
    down_out[...] = down[...]


def solution(mesh):
    n = mesh.shape["dp"]
    in_specs = (
        P(("groups", "dp"), None),
        P(("groups", "dp")),
        P(),
        P(),
        P(),
        P(),
        P("groups", "dp"),
        P("dp", None),
        P("groups", None),
        P(),
    )
    out_specs = (
        P("groups"),
        P(("groups", "dp"), None),
        P(("groups", "dp"), None),
        P(("groups", "dp"), None),
    )

    def per_device(
        states, lengths, norm_gain, w_gate, w_up, w_down, context, w_out, resid_stream, teacher_gain
    ):
        tokens, model = states.shape
        hidden_width = w_gate.shape[1]
        docs_dev = lengths.shape[0]
        docs = context.shape[0]
        teacher_width = w_out.shape[1]
        feat = teacher_width // n
        rows = model // n
        width = 256
        chunks = 2 * hidden_width // width
        cols = n // 4
        fold = max(1, 128 // docs)
        packed = model + 128
        hbm = pl.BlockSpec(memory_space=pl.ANY)
        vmem = pl.BlockSpec(memory_space=pltpu.VMEM)
        sem = pltpu.SemaphoreType.DMA
        loss, grad_gate, grad_up, grad_down = pl.pallas_call(
            functools.partial(step_kernel, n, width),
            out_shape=(
                jax.ShapeDtypeStruct((1, 1), F32),
                jax.ShapeDtypeStruct((rows, hidden_width), F32),
                jax.ShapeDtypeStruct((rows, hidden_width), F32),
                jax.ShapeDtypeStruct((hidden_width // n, model), F32),
            ),
            in_specs=[hbm, pl.BlockSpec(memory_space=pltpu.SMEM), vmem] + [hbm] * 6 + [vmem],
            out_specs=(vmem,) * 4,
            scratch_shapes=[
                pltpu.VMEM((tokens, model), BF16),
                pltpu.VMEM((model, hidden_width), BF16),
                pltpu.VMEM((model, hidden_width), BF16),
                pltpu.VMEM((hidden_width, model), BF16),
                pltpu.VMEM(context.shape, BF16),
                pltpu.VMEM(w_out.shape, BF16),
                pltpu.VMEM(resid_stream.shape, BF16),
                pltpu.VMEM((n, docs, feat), BF16),
                pltpu.VMEM((n, docs, feat), BF16),
                pltpu.VMEM((n, docs // fold, docs * fold), F32),
                pltpu.VMEM((n, docs_dev, packed), F32),
                pltpu.VMEM((n, docs_dev, hidden_width), F32),
                pltpu.VMEM((docs_dev, model), F32),
                pltpu.VMEM((docs, packed), F32),
                pltpu.VMEM((docs, hidden_width), F32),
                pltpu.VMEM((cols, 2, 2, rows, tokens), BF16),
                pltpu.VMEM((cols, 2, rows, tokens), BF16),
                pltpu.VMEM((2, chunks, tokens, width), BF16),
                pltpu.VMEM((chunks, 16, width), F32),
                pltpu.VMEM((chunks, cols // 2, 2, rows, width), BF16),
                pltpu.VMEM((chunks, cols // 2, 2, rows, width), F32),
                pltpu.VMEM((chunks, cols // 2, 2, rows, width), BF16),
                pltpu.VMEM((chunks, cols // 2, rows, width), BF16),
                pltpu.VMEM((chunks, cols // 2, rows, width), BF16),
                pltpu.VMEM((chunks, cols // 2, rows, width), BF16),
                pltpu.VMEM((chunks, cols // 2, rows, width), BF16),
                pltpu.VMEM((chunks, rows, width), F32),
                sem((5,)), sem((2, chunks // 2)),
                sem((n,)), sem((n,)), sem((n,)), sem((n,)), sem((n,)), sem((n,)), sem((n,)), sem((n,)),
                sem((chunks + 1,)), sem((chunks + 1,)),
                sem((chunks,)), sem((chunks,)), sem((chunks,)), sem((chunks,)),
                sem((chunks, cols // 2)), sem((chunks, cols // 2)),
            ],
            compiler_params=pltpu.CompilerParams(
                collective_id=0, has_side_effects=True, vmem_limit_bytes=60 * 1024 * 1024
            ),
        )(
            states, lengths, norm_gain, w_gate, w_up, w_down, context, w_out,
            resid_stream, teacher_gain,
        )
        made = (grad_gate, grad_up, grad_down)
        made = pl.pallas_call(
            hand_over,
            out_shape=tuple(jax.ShapeDtypeStruct(g.shape, g.dtype) for g in made),
            in_specs=[vmem] * 3,
            out_specs=(vmem,) * 3,
        )(*made)
        return (loss.reshape(1), *made)

    return jax.shard_map(
        per_device, mesh=mesh, in_specs=in_specs, out_specs=out_specs, check_vma=False
    )
```
